512 devices in a mesh: dom: 8 (over y), dp: 64 (over z, x, core).
Axes of the slice: x: 4, y: 8, z: 8, core: 2. Of those that a mesh axis runs over, the one named last changes fastest.
Arguments:
- positions: float32 [512, 32768], P('dom', 'dp'), may hold values from -6 to 6
- ancestors: int32 [512], P('dom'), may hold values from 0 to 511
- block_choice: int32 [64, 64], replicated, may hold values from 0 to 3
- tile_slot: int32 [1024, 8], P('dp'), may hold values from 0 to 63, all different within a row
- design: bfloat16 [131072, 1024], P('dp'), may hold values from -0.1875 to 0.1875
- labels: int32 [131072], P('dp'), may hold values 0 or 1
- row_section: int32 [131072], P('dp'), may hold values from 0 to 4
Outputs:
- advanced: float32 [512, 32768], P('dom', 'dp')
- mean_loglik: float32 [512], P('dom')
The draws below stay inside these ranges and needn't reach their ends.
Inputs may be any that keep to these rules, and one draw needn't show every extreme that they name: Each row of tile_slot names 8 different owners.
All inputs are finite; a program needn't handle non-finite values. No bound on the sum of `labels` on one device may be relied on, other than what follows from the above.
Results may differ from the reference program's by a relative error of at most 0.00048.
Values may be sent and summed in bfloat16 or wider, within the bound.
No kernel may reach another device: no remote copies, remote signals or barrier semaphores. Data moves between devices by JAX's collectives and lax.ppermute only.
A program may use at most 64 MiB of HBM per device.

```python
import jax
import jax.numpy as jnp
from jax import lax

F = 32768
TILE = 128
K = 8
SECTIONS = 5
CURRENT = 2
RB_DEV = 16
P_SIZE = 512
ROWS = 131072
BLK_OWN = 4
N_DP = 64


def place_ends(entries, own_key, low, high):
    dims = entries.shape
    index_at = [jax.random.randint(jax.random.fold_in(own_key, axis), (), 0, dims[axis]) for axis in range(len(dims))]
    entries = entries.at[tuple(index_at)].set(low)
    longest = dims.index(max(dims))
    index_at[longest] = (index_at[longest] + 1) % dims[longest]
    return entries.at[tuple(index_at)].set(high)


def level_of(stream_key, shape, cuts, least, top_value):
    factor_of, own = 1.0, jax.random.fold_in(stream_key, 6)
    for position, blocks in cuts:
        draws = jnp.exp(jax.random.uniform(jax.random.fold_in(own, position), (blocks,), jnp.float32, least / len(cuts), top_value / len(cuts)))
        factor_of = factor_of * jnp.repeat(draws, shape[position] // blocks).reshape([-1 if axis == position else 1 for axis in range(len(shape))])
    return factor_of


def different_ones(rng, rows, count, top, lift):
    order = jax.random.permutation(jax.random.fold_in(rng, 1), count)
    favour = order
    for power in range(3):
        favour = favour * favour // count
    favour = favour * lift // count
    lots = jax.random.randint(jax.random.fold_in(rng, 2), (rows, count), 0, 4096) + favour
    holders = jax.random.permutation(jax.random.fold_in(rng, 3), rows)[jnp.arange(count) % rows]
    lots = jnp.where(jnp.arange(rows)[:, None] == holders[None, :], 1 << 14, lots)
    priority = lots * count + jnp.arange(count)
    return lax.top_k(priority.astype(jnp.int32), top)[1].astype(jnp.int32)


def normal_values(stream_key, dims, width, bound, split=(), held_as=jnp.bfloat16):
    array = jax.random.normal(stream_key, dims, jnp.float32) * width
    if len(split) > 0:
        array = level_of(stream_key, dims, split, -0.22, 0.18) * array
    return jnp.clip(array, min=-bound, max=bound).astype(held_as)


def setup_inputs(seed: int = 0) -> dict:
    keys = jax.random.split(jax.random.key(seed), 8)
    positions = normal_values(keys[0], (P_SIZE, F), 1.0, 6.0, ((0, 8), (1, 64)), jnp.float32)
    ancestors = place_ends(jax.random.randint(keys[1], (P_SIZE,), 0, P_SIZE), jax.random.fold_in(keys[1], 1), 0, P_SIZE - 1).astype(jnp.int32)
    block_choice = place_ends(jax.random.randint(keys[2], (N_DP, N_DP), 0, BLK_OWN), jax.random.fold_in(keys[2], 1), 0, BLK_OWN - 1).astype(jnp.int32)
    tile_slot = different_ones(keys[3], (RB_DEV * N_DP), N_DP, K, 1024)
    design = normal_values(keys[4], (ROWS, K * TILE), (K * TILE) ** -0.5, 0.1875, ((0, 64),))
    labels = place_ends((jax.random.randint(keys[5], (ROWS,), 0, 2) < 1).astype(jnp.int32), jax.random.fold_in(keys[5], 1), 0, 1)
    row_section = place_ends(jax.random.randint(keys[6], (ROWS,), 0, SECTIONS), jax.random.fold_in(keys[6], 1), 0, SECTIONS - 1).astype(jnp.int32)
    return dict(positions=positions, ancestors=ancestors, block_choice=block_choice, tile_slot=tile_slot, design=design, labels=labels, row_section=row_section)


step_size = 1.0
prior_precision = 0.05


def tile_logits(narrow, design_tiles, blocks):
    weights = jnp.take(narrow, blocks, axis=1).astype(jnp.float32)
    return jnp.einsum('bikc,pbkc->bpi', design_tiles.astype(jnp.float32), weights)


def reference(positions, ancestors, block_choice, tile_slot, design, labels, row_section):
    blocks_owned = F // (TILE * N_DP)
    blocks_dev = tile_slot.shape[0] // N_DP
    particle_count = positions.shape[0]
    resampled = jnp.take(positions, ancestors, axis=0)
    design_all = design.reshape(N_DP, blocks_dev, TILE, K, TILE)
    slots = tile_slot.reshape(N_DP, blocks_dev, K)
    owner_pick = block_choice[jnp.arange(N_DP)[:, None, None], slots]
    feature_blocks = (slots * blocks_owned + owner_pick).astype(jnp.int32)
    targets = labels.reshape(N_DP, blocks_dev, 1, TILE).astype(jnp.float32)
    sections = row_section.reshape(N_DP, blocks_dev, 1, TILE)
    narrow = resampled.astype(jnp.bfloat16).reshape(particle_count, F // TILE, TILE)

    def add_gradient(total, packed):
        design_tiles, blocks, target_rows, section_rows = packed
        logits = tile_logits(narrow, design_tiles, blocks)
        residual = jnp.where(section_rows <= CURRENT, target_rows - jax.nn.sigmoid(logits), 0.0).astype(jnp.bfloat16)
        per_tile = jnp.einsum('bpi,bikc->pbkc', residual.astype(jnp.float32), design_tiles.astype(jnp.float32))
        return total.at[:, blocks].add(per_tile), None

    gradient_start = jnp.zeros((particle_count, F // TILE, TILE), jnp.float32)
    gradient, unused = lax.scan(add_gradient, gradient_start, (design_all, feature_blocks, targets, sections))
    advanced = resampled + step_size * (gradient.reshape(particle_count, F) - prior_precision * resampled)
    narrow_new = advanced.astype(jnp.bfloat16).reshape(particle_count, F // TILE, TILE)

    def add_likelihood(carry, packed):
        totals, counted = carry
        design_tiles, blocks, target_rows, section_rows = packed
        logits = tile_logits(narrow_new, design_tiles, blocks)
        chosen = section_rows == CURRENT + 1
        loglik = jnp.where(chosen, target_rows * logits - jax.nn.softplus(logits), 0.0)
        return (totals + jnp.sum(loglik, axis=(0, 2)), counted + jnp.sum(chosen.astype(jnp.float32))), None

    start = (jnp.zeros((particle_count,), jnp.float32), jnp.zeros((), jnp.float32))
    (totals, counted), unused = lax.scan(add_likelihood, start, (design_all, feature_blocks, targets, sections))
    return advanced, totals / jnp.maximum(counted, 1.0)
```

```python
import functools

import jax
import jax.numpy as jnp
from jax import lax
from jax.experimental import pallas as pl
from jax.experimental.pallas import tpu as pltpu
from jax.sharding import Mesh, PartitionSpec as P

TILE = 128
CURRENT = 2
step_size = 1.0
prior_precision = 0.05

f32 = jnp.float32
bf16 = jnp.bfloat16
f16 = jnp.float16

VMEM = pltpu.VMEM
SMEM = pltpu.SMEM


def vspec():
    return pl.BlockSpec(memory_space=VMEM)


def sspec():
    return pl.BlockSpec(memory_space=SMEM)


def params(mib):
    return pltpu.CompilerParams(vmem_limit_bytes=mib << 20)


def exchange(x, axes):
    return lax.all_to_all(x, axes, split_axis=0, concat_axis=0, tiled=True)


def resample_kernel(anc, row, lineage, resampled, outgoing, blocks):
    particles, width = resampled.shape
    owned = width // TILE

    def pick(i, carry):
        resampled[pl.ds(i, 1), :] = lineage[pl.ds(anc[i], 1), :]
        return carry

    lax.fori_loop(0, particles, pick, 0, unroll=8)
    for q in range(owned):
        blocks[q] = resampled[:, q * TILE : (q + 1) * TILE].astype(bf16)

    def send(d, carry):
        outgoing[d] = blocks[row[d]]
        return carry

    lax.fori_loop(0, outgoing.shape[0], send, 0, unroll=8)


def weights_of(slot, fetched, b, per_block):
    return jnp.concatenate([fetched[slot[b, k]] for k in range(per_block)], axis=1)


def logits_of(weights, tiles):
    return lax.dot_general(
        weights, tiles, (((1,), (1,)), ((), ())), preferred_element_type=f32
    )


def design_copy(design, held, sems, b):
    rows = pl.ds(pl.multiple_of(b * TILE, TILE), TILE)
    return pltpu.make_async_copy(design.at[rows], held.at[rows], sems.at[b])


def gradient_kernel(slot, design, fetched, labels, sections, outgoing, total, held, sems):
    row_blocks, per_block = slot.shape
    for b in range(row_blocks):
        design_copy(design, held, sems, b).start()
    total[...] = jnp.zeros_like(total)

    def block(b, carry):
        design_copy(design, held, sems, b).wait()
        tiles = held[pl.ds(pl.multiple_of(b * TILE, TILE), TILE), :]
        logits = logits_of(weights_of(slot, fetched, b, per_block), tiles)
        target = labels[pl.ds(b, 1), :].astype(f32)
        active = sections[pl.ds(b, 1), :] <= CURRENT
        residual = jnp.where(active, target - jax.nn.sigmoid(logits), 0.0).astype(bf16)
        terms = jnp.dot(residual, tiles, preferred_element_type=f32)
        for k in range(per_block):
            j = slot[b, k]
            total[j] += terms[:, k * TILE : (k + 1) * TILE]
        return carry

    lax.fori_loop(0, row_blocks, block, 0)
    outgoing[...] = total[...]


def advance_kernel(row, column, resampled, incoming, advanced, outgoing, total, blocks):
    particles, width = resampled.shape
    owned = width // TILE
    total[...] = jnp.zeros_like(total)

    def add(s, carry):
        q = column[s]
        total[q] += incoming[s].astype(f32)
        return carry

    lax.fori_loop(0, incoming.shape[0], add, 0, unroll=4)
    for q in range(owned):
        lanes = slice(q * TILE, (q + 1) * TILE)
        old = resampled[:, lanes]
        new = old + step_size * (total[q] - prior_precision * old)
        advanced[:, lanes] = new
        blocks[q] = new.astype(bf16)

    def send(d, carry):
        outgoing[d] = blocks[row[d]]
        return carry

    lax.fori_loop(0, outgoing.shape[0], send, 0, unroll=8)


def likelihood_kernel(slot, design, fetched, labels, sections, outgoing, held, sems):
    row_blocks, per_block = slot.shape
    particles = fetched.shape[1]
    for b in range(row_blocks):
        design_copy(design, held, sems, b).start()

    def block(b, carry):
        total, counted = carry
        design_copy(design, held, sems, b).wait()
        tiles = held[pl.ds(pl.multiple_of(b * TILE, TILE), TILE), :]
        logits = logits_of(weights_of(slot, fetched, b, per_block), tiles)
        target = labels[pl.ds(b, 1), :].astype(f32)
        chosen = sections[pl.ds(b, 1), :] == CURRENT + 1
        soft = jnp.maximum(logits, 0.0) + jnp.log1p(jnp.exp(-jnp.abs(logits)))
        total += jnp.where(chosen, target * logits - soft, 0.0)
        counted += chosen.astype(f32)
        return total, counted

    total, counted = lax.fori_loop(
        0,
        row_blocks,
        block,
        (jnp.zeros((particles, TILE), f32), jnp.zeros((1, TILE), f32)),
    )
    rows = jnp.concatenate([total, jnp.broadcast_to(counted, (TILE - particles, TILE))], axis=0)
    sums = jnp.sum(rows.T, axis=0, keepdims=True)
    outgoing[...] = jnp.broadcast_to(sums[None], outgoing.shape)


def shards(data_axes, positions, ancestors, block_choice, tile_slot, design, labels, row_section):
    data_width = lax.axis_size(data_axes)
    device_index = lax.axis_index(data_axes)
    groups = lax.axis_size("dom")
    particles, width = positions.shape
    owned = width // TILE
    row_blocks, per_block = tile_slot.shape
    column = lax.dynamic_index_in_dim(block_choice, device_index, 1, keepdims=False)
    labels = labels.reshape(row_blocks, TILE)
    sections = row_section.reshape(row_blocks, TILE)

    spread = jnp.broadcast_to(positions[None], (groups, particles, width))
    lineage = exchange(spread, "dom").reshape(groups * particles, width)
    block_shape = (data_width, particles, TILE)
    resampled, outgoing = pl.pallas_call(
        resample_kernel,
        out_shape=(
            jax.ShapeDtypeStruct((particles, width), f32),
            jax.ShapeDtypeStruct(block_shape, bf16),
        ),
        in_specs=[sspec(), sspec(), vspec()],
        out_specs=(vspec(), vspec()),
        scratch_shapes=[VMEM((owned, particles, TILE), bf16)],
        compiler_params=params(8),
    )(ancestors, column, lineage)
    fetched = exchange(outgoing, data_axes)
    terms = pl.pallas_call(
        gradient_kernel,
        out_shape=jax.ShapeDtypeStruct(block_shape, f32),
        in_specs=[sspec(), pl.BlockSpec(memory_space=pl.ANY), vspec(), vspec(), vspec()],
        out_specs=vspec(),
        scratch_shapes=[
            VMEM(block_shape, f32),
            VMEM(design.shape, bf16),
            pltpu.SemaphoreType.DMA((row_blocks,)),
        ],
        compiler_params=params(16),
    )(tile_slot, design, fetched, labels, sections)
    incoming = exchange(terms.astype(f16), data_axes).astype(f32)
    advanced, outgoing = pl.pallas_call(
        advance_kernel,
        out_shape=(
            jax.ShapeDtypeStruct((particles, width), f32),
            jax.ShapeDtypeStruct(block_shape, bf16),
        ),
        in_specs=[sspec(), sspec(), vspec(), vspec()],
        out_specs=(vspec(), vspec()),
        scratch_shapes=[
            VMEM((owned, particles, TILE), f32),
            VMEM((owned, particles, TILE), bf16),
        ],
        compiler_params=params(8),
    )(column, column, resampled, incoming)
    fetched_new = exchange(outgoing, data_axes)
    sums = pl.pallas_call(
        likelihood_kernel,
        out_shape=jax.ShapeDtypeStruct((data_width, 1, TILE), f32),
        in_specs=[sspec(), pl.BlockSpec(memory_space=pl.ANY), vspec(), vspec(), vspec()],
        out_specs=vspec(),
        scratch_shapes=[
            VMEM(design.shape, bf16),
            pltpu.SemaphoreType.DMA((row_blocks,)),
        ],
        compiler_params=params(12),
    )(tile_slot, design, fetched_new, labels, sections)
    sums = jnp.sum(exchange(sums, data_axes), axis=(0, 1))
    return advanced, sums[:particles] / jnp.maximum(sums[particles], 1.0)


def solution(mesh):
    return jax.shard_map(
        functools.partial(shards, "dp"),
        mesh=mesh,
        in_specs=(P("dom", "dp"), P("dom"), P(), P("dp", None), P("dp", None), P("dp"), P("dp")),
        out_specs=(P("dom", "dp"), P("dom")),
        check_vma=False,
    )
```

```python
import jax
import jax.numpy as jnp
from jax import lax
from jax.experimental import pallas as pl
from jax.experimental.pallas import tpu as pltpu
from jax.sharding import PartitionSpec as P


TILE = 128
CURRENT = 2
CHUNKS = 4
step_size = 1.0
prior_precision = 0.05

f32 = jnp.float32
bf16 = jnp.bfloat16
f16 = jnp.float16

VMEM = pltpu.VMEM
SMEM = pltpu.SMEM


def vspec():
    return pl.BlockSpec(memory_space=VMEM)


def sspec():
    return pl.BlockSpec(memory_space=SMEM)


def params(mib):
    return pltpu.CompilerParams(vmem_limit_bytes=mib << 20)


def exchange(x, axes):
    return lax.all_to_all(x, axes, split_axis=0, concat_axis=0, tiled=True)


def send_blocks(me, choice, blocks, outgoing):
    def send(d, carry):
        outgoing[d] = blocks[choice[d, me[0]]]
        return carry

    lax.fori_loop(0, outgoing.shape[0], send, 0, unroll=8)


def select_kernel(me, choice, positions, outgoing, blocks):
    for q in range(blocks.shape[0]):
        blocks[q] = positions[:, q * TILE : (q + 1) * TILE].astype(bf16)
    send_blocks(me, choice, blocks, outgoing)


def weights_of(slot, fetched, b, per_block):
    return jnp.concatenate([fetched[slot[b, k]] for k in range(per_block)], axis=1)


def logits_of(weights, tiles):
    return lax.dot_general(
        weights, tiles, (((1,), (1,)), ((), ())), preferred_element_type=f32
    )


def chunk_copies(design, held, sems):
    rows = design.shape[0] // CHUNKS
    return [
        pltpu.make_async_copy(
            design.at[pl.ds(c * rows, rows)], held.at[pl.ds(c * rows, rows)], sems.at[c]
        )
        for c in range(CHUNKS)
    ]


def gradient_kernel(slot, design, fetched, labels, sections, outgoing, held, sems):
    row_blocks, per_block = slot.shape
    copies = chunk_copies(design, held, sems)
    for copy in copies:
        copy.start()
    outgoing[...] = jnp.zeros_like(outgoing)

    for b in range(row_blocks):
        if b % (row_blocks // CHUNKS) == 0:
            copies[b // (row_blocks // CHUNKS)].wait()
        tiles = held[b * TILE : (b + 1) * TILE, :]
        logits = logits_of(weights_of(slot, fetched, b, per_block), tiles)
        target = labels[b : b + 1, :].astype(f32)
        active = sections[b : b + 1, :] <= CURRENT
        residual = jnp.where(active, target - jax.nn.sigmoid(logits), 0.0).astype(bf16)
        terms = jnp.dot(residual, tiles, preferred_element_type=f32)
        for k in range(per_block):
            j = slot[b, k]
            outgoing[j] += terms[:, k * TILE : (k + 1) * TILE]


def advance_kernel(me, choice, positions, incoming, advanced, outgoing, total, blocks):
    total[...] = jnp.zeros_like(total)

    def add(s, carry):
        total[choice[s, me[0]]] += incoming[s].astype(f32)
        return carry

    lax.fori_loop(0, incoming.shape[0], add, 0, unroll=4)
    for q in range(blocks.shape[0]):
        lanes = slice(q * TILE, (q + 1) * TILE)
        old = positions[:, lanes]
        new = old + step_size * (total[q] - prior_precision * old)
        advanced[:, lanes] = new
        blocks[q] = new.astype(bf16)
    send_blocks(me, choice, blocks, outgoing)


def pick_kernel(group, ancestors, *refs):
    moved, (resampled, table, sems) = refs[:-3], refs[-3:]
    particles = resampled.shape[0]
    groups = len(moved)
    copies = [
        pltpu.make_async_copy(moved[k], table.at[pl.ds(k * particles, particles)], sems.at[k])
        for k in range(groups)
    ]
    for copy in copies:
        copy.start()
    for copy in copies:
        copy.wait()

    def pick(i, carry):
        a = ancestors[i]
        ahead = lax.rem(group[0] - lax.div(a, particles) + groups, groups)
        row = ahead * particles + lax.rem(a, particles)
        resampled[pl.ds(i, 1), :] = table[pl.ds(row, 1), :]
        return carry

    lax.fori_loop(0, particles, pick, 0, unroll=8)


def likelihood_kernel(slot, design, fetched, labels, sections, outgoing, held, sems):
    row_blocks, per_block = slot.shape
    particles = fetched.shape[1]
    copies = chunk_copies(design, held, sems)
    for copy in copies:
        copy.start()
    total = jnp.zeros((particles, TILE), f32)
    counted = jnp.zeros((1, TILE), f32)
    for b in range(row_blocks):
        if b % (row_blocks // CHUNKS) == 0:
            copies[b // (row_blocks // CHUNKS)].wait()
        tiles = held[b * TILE : (b + 1) * TILE, :]
        logits = logits_of(weights_of(slot, fetched, b, per_block), tiles)
        target = labels[b : b + 1, :].astype(f32)
        chosen = sections[b : b + 1, :] == CURRENT + 1
        soft = jnp.maximum(logits, 0.0) + jnp.log1p(jnp.exp(-jnp.abs(logits)))
        total += jnp.where(chosen, target * logits - soft, 0.0)
        counted += chosen.astype(f32)
    rows = jnp.concatenate([total, jnp.broadcast_to(counted, (TILE - particles, TILE))], axis=0)
    sums = jnp.sum(rows.T, axis=0, keepdims=True)
    outgoing[...] = jnp.broadcast_to(sums[None], outgoing.shape)


def shards(positions, ancestors, block_choice, tile_slot, design, labels, row_section):
    data_width = lax.axis_size("dp")
    groups = lax.axis_size("dom")
    me = lax.axis_index("dp").astype(jnp.int32).reshape(1)
    group = lax.axis_index("dom").astype(jnp.int32).reshape(1)
    particles, width = positions.shape
    owned = width // TILE
    row_blocks, _ = tile_slot.shape
    labels = labels.reshape(row_blocks, TILE)
    sections = row_section.reshape(row_blocks, TILE)
    block_shape = (data_width, particles, TILE)
    design = pltpu.with_memory_space_constraint(design, pltpu.HBM)

    outgoing = pl.pallas_call(
        select_kernel,
        out_shape=jax.ShapeDtypeStruct(block_shape, bf16),
        in_specs=[sspec(), sspec(), vspec()],
        out_specs=vspec(),
        scratch_shapes=[VMEM((owned, particles, TILE), bf16)],
        compiler_params=params(4),
    )(me, block_choice, positions)
    fetched = exchange(outgoing, "dp")
    terms = pl.pallas_call(
        gradient_kernel,
        out_shape=jax.ShapeDtypeStruct(block_shape, f32),
        in_specs=[sspec(), pl.BlockSpec(memory_space=pltpu.HBM), vspec(), vspec(), vspec()],
        out_specs=vspec(),
        scratch_shapes=[VMEM(design.shape, bf16), pltpu.SemaphoreType.DMA((CHUNKS,))],
        compiler_params=params(12),
    )(tile_slot, design, fetched, labels, sections)
    incoming = exchange(terms.astype(f16), "dp").astype(f32)
    moved, outgoing = pl.pallas_call(
        advance_kernel,
        out_shape=(
            jax.ShapeDtypeStruct((particles, width), f32),
            jax.ShapeDtypeStruct(block_shape, bf16),
        ),
        in_specs=[sspec(), sspec(), vspec(), vspec()],
        out_specs=(vspec(), vspec()),
        scratch_shapes=[
            VMEM((owned, particles, TILE), f32),
            VMEM((owned, particles, TILE), bf16),
        ],
        compiler_params=params(6),
    )(me, block_choice, positions, incoming)
    fetched_new = exchange(outgoing, "dp")
    everyone = [moved]
    for ahead in range(1, groups):
        ring = [(g, (g + ahead) % groups) for g in range(groups)]
        everyone.append(lax.ppermute(moved, "dom", ring))
    sums = pl.pallas_call(
        likelihood_kernel,
        out_shape=jax.ShapeDtypeStruct((data_width, 1, TILE), f32),
        in_specs=[sspec(), pl.BlockSpec(memory_space=pltpu.HBM), vspec(), vspec(), vspec()],
        out_specs=vspec(),
        scratch_shapes=[VMEM(design.shape, bf16), pltpu.SemaphoreType.DMA((CHUNKS,))],
        compiler_params=params(12),
    )(tile_slot, design, fetched_new, labels, sections)
    sums = jnp.sum(exchange(sums, "dp"), axis=0)
    spread = jnp.broadcast_to(sums[None], (groups, 1, TILE))
    table = exchange(spread, "dom")[:, 0]
    advanced = pl.pallas_call(
        pick_kernel,
        out_shape=jax.ShapeDtypeStruct((particles, width), f32),
        in_specs=[sspec(), sspec()] + [vspec()] * groups,
        out_specs=vspec(),
        scratch_shapes=[VMEM((groups * particles, width), f32), pltpu.SemaphoreType.DMA((groups,))],
        compiler_params=params(4),
    )(group, ancestors, *everyone)
    from_group = jnp.arange(groups)[None, :, None] == (ancestors // particles)[:, None, None]
    from_row = jnp.arange(TILE)[None, None, :] == (ancestors % particles)[:, None, None]
    totals = jnp.sum(jnp.where(from_group & from_row, table[None], 0.0), axis=(1, 2))
    return advanced, totals / jnp.maximum(sums[0, particles], 1.0)


def solution(mesh):
    return jax.shard_map(
        shards,
        mesh=mesh,
        in_specs=(P("dom", "dp"), P("dom"), P(), P("dp", None), P("dp", None), P("dp"), P("dp")),
        out_specs=(P("dom", "dp"), P("dom")),
        check_vma=False,
    )
```

```python
import functools

import jax
import jax.numpy as jnp
from jax import lax
from jax.experimental import pallas as pl
from jax.experimental.pallas import tpu as pltpu
from jax.sharding import PartitionSpec as P


TILE = 128
CURRENT = 2
CHUNKS = 4
step_size = 1.0
prior_precision = 0.05

f32 = jnp.float32
bf16 = jnp.bfloat16
f16 = jnp.float16

VMEM = pltpu.VMEM
SMEM = pltpu.SMEM


def vspec():
    return pl.BlockSpec(memory_space=VMEM)


def sspec():
    return pl.BlockSpec(memory_space=SMEM)


def hspec():
    return pl.BlockSpec(memory_space=pltpu.HBM)


def params(mib):
    return pltpu.CompilerParams(vmem_limit_bytes=mib << 20)


def exchange(x, axes):
    return lax.all_to_all(x, axes, split_axis=0, concat_axis=0, tiled=True)


def select_kernel(me, choice, positions, outgoing, column, choice_here, here, blocks, sems):
    first = pltpu.make_async_copy(choice, choice_here, sems.at[0])
    second = pltpu.make_async_copy(positions, here, sems.at[1])
    first.start()
    second.start()
    second.wait()
    for q in range(blocks.shape[0]):
        blocks[q] = here[:, q * TILE : (q + 1) * TILE].astype(bf16)
    first.wait()

    def send(d, carry):
        chosen = choice_here[d, me[0]]
        column[d] = chosen
        outgoing[d] = blocks[chosen]
        return carry

    lax.fori_loop(0, outgoing.shape[0], send, 0, unroll=8)


def weights_of(slot, fetched, b, per_block):
    return jnp.concatenate([fetched[slot[k, b]] for k in range(per_block)], axis=1)


def logits_of(weights, tiles):
    return lax.dot_general(
        weights, tiles, (((1,), (1,)), ((), ())), preferred_element_type=f32
    )


def chunk_copies(design, held, sems):
    chunks = sems.shape[0]
    rows = design.shape[0] // chunks
    return [
        pltpu.make_async_copy(
            design.at[pl.ds(c * rows, rows)], held.at[pl.ds(c * rows, rows)], sems.at[c]
        )
        for c in range(chunks)
    ]


def gradient_kernel(slot, design, fetched, labels, sections, outgoing, held, sems):
    per_block, row_blocks = slot.shape
    copies = chunk_copies(design, held, sems)
    for copy in copies:
        copy.start()
    outgoing[...] = jnp.zeros_like(outgoing)

    def tiles_of(b):
        return held[b * TILE : (b + 1) * TILE, :]

    residuals = []
    for b in range(row_blocks):
        if b % (row_blocks // len(copies)) == 0:
            copies[b // (row_blocks // len(copies))].wait()
        logits = logits_of(weights_of(slot, fetched, b, per_block), tiles_of(b))
        target = labels[b : b + 1, :].astype(f32)
        active = sections[b : b + 1, :] <= CURRENT
        residual = jnp.where(active, target - jax.nn.sigmoid(logits), 0.0)
        residuals.append(residual.astype(bf16))
    for b in range(row_blocks):
        terms = jnp.dot(residuals[b], tiles_of(b), preferred_element_type=f32)
        for k in range(per_block):
            j = slot[k, b]
            outgoing[j] += terms[:, k * TILE : (k + 1) * TILE]


def advance_kernel(column, positions, incoming, advanced, outgoing, here, total, blocks, sem):
    copy = pltpu.make_async_copy(positions, here, sem)
    copy.start()
    total[...] = jnp.zeros_like(total)

    def add(s, carry):
        total[column[s]] += incoming[s].astype(f32)
        return carry

    lax.fori_loop(0, incoming.shape[0], add, 0, unroll=4)
    copy.wait()
    for q in range(blocks.shape[0]):
        lanes = slice(q * TILE, (q + 1) * TILE)
        old = here[:, lanes]
        new = old + step_size * (total[q] - prior_precision * old)
        advanced[:, lanes] = new
        blocks[q] = new.astype(bf16)

    def send(d, carry):
        outgoing[d] = blocks[column[d]]
        return carry

    lax.fori_loop(0, outgoing.shape[0], send, 0, unroll=8)


def pick_kernel(group, ancestors, *refs):
    moved, (resampled, table, sems) = refs[:-3], refs[-3:]
    particles = resampled.shape[0]
    groups = len(moved)
    copies = [
        pltpu.make_async_copy(moved[k], table.at[pl.ds(k * particles, particles)], sems.at[k])
        for k in range(groups)
    ]
    for copy in copies:
        copy.start()
    for copy in copies:
        copy.wait()

    def pick(i, carry):
        a = ancestors[i]
        ahead = lax.rem(group[0] - lax.div(a, particles) + groups, groups)
        row = ahead * particles + lax.rem(a, particles)
        resampled[pl.ds(i, 1), :] = table[pl.ds(row, 1), :]
        return carry

    lax.fori_loop(0, particles, pick, 0, unroll=8)


def likelihood_kernel(slot, design, fetched, labels, sections, outgoing, held, sems):
    per_block, row_blocks = slot.shape
    particles = fetched.shape[1]
    copies = chunk_copies(design, held, sems)
    for copy in copies:
        copy.start()
    total = jnp.zeros((particles, TILE), f32)
    counted = jnp.zeros((1, TILE), f32)
    for b in range(row_blocks):
        if b % (row_blocks // len(copies)) == 0:
            copies[b // (row_blocks // len(copies))].wait()
        tiles = held[b * TILE : (b + 1) * TILE, :]
        logits = logits_of(weights_of(slot, fetched, b, per_block), tiles)
        target = labels[b : b + 1, :].astype(f32)
        chosen = sections[b : b + 1, :] == CURRENT + 1
        soft = jnp.maximum(logits, 0.0) + jnp.log1p(jnp.exp(-jnp.abs(logits)))
        total += jnp.where(chosen, target * logits - soft, 0.0)
        counted += chosen.astype(f32)
    rows = jnp.concatenate([total, jnp.broadcast_to(counted, (TILE - particles, TILE))], axis=0)
    sums = jnp.sum(rows.T, axis=0, keepdims=True)
    outgoing[...] = jnp.broadcast_to(sums[None], outgoing.shape)


def mean_kernel(particles, sums, means):
    total = jnp.sum(sums[...], axis=0)
    count = jnp.maximum(total[:, particles : particles + 1], 1.0)
    means[...] = jnp.broadcast_to((total / count)[None], means.shape)


def shards(positions, ancestors, block_choice, tile_slot, design, labels, row_section):
    data_width = lax.axis_size("dp")
    groups = lax.axis_size("dom")
    me = lax.axis_index("dp").astype(jnp.int32).reshape(1)
    group = lax.axis_index("dom").astype(jnp.int32).reshape(1)
    particles, width = positions.shape
    owned = width // TILE
    row_blocks = tile_slot.shape[0]
    labels = labels.reshape(row_blocks, TILE)
    sections = row_section.reshape(row_blocks, TILE)
    block_shape = (data_width, particles, TILE)
    slot = tile_slot.T
    design = pltpu.with_memory_space_constraint(design, pltpu.HBM)

    positions = pltpu.with_memory_space_constraint(positions, pltpu.HBM)
    chosen = pltpu.with_memory_space_constraint(block_choice, pltpu.HBM)
    outgoing, column = pl.pallas_call(
        select_kernel,
        out_shape=(
            jax.ShapeDtypeStruct(block_shape, bf16),
            jax.ShapeDtypeStruct((data_width,), jnp.int32),
        ),
        in_specs=[sspec(), hspec(), hspec()],
        out_specs=(vspec(), sspec()),
        scratch_shapes=[
            SMEM(block_choice.shape, jnp.int32),
            VMEM((particles, width), f32),
            VMEM((owned, particles, TILE), bf16),
            pltpu.SemaphoreType.DMA((2,)),
        ],
        compiler_params=params(4),
    )(me, chosen, positions)
    fetched = exchange(outgoing, "dp")
    terms = pl.pallas_call(
        gradient_kernel,
        out_shape=jax.ShapeDtypeStruct(block_shape, f32),
        in_specs=[sspec(), hspec(), vspec(), vspec(), vspec()],
        out_specs=vspec(),
        scratch_shapes=[VMEM(design.shape, bf16), pltpu.SemaphoreType.DMA((CHUNKS,))],
        compiler_params=params(12),
    )(slot, design, fetched, labels, sections)
    incoming = exchange(terms.astype(f16), "dp").astype(f32)
    moved, outgoing = pl.pallas_call(
        advance_kernel,
        out_shape=(
            jax.ShapeDtypeStruct((particles, width), f32),
            jax.ShapeDtypeStruct(block_shape, bf16),
        ),
        in_specs=[sspec(), hspec(), vspec()],
        out_specs=(vspec(), vspec()),
        scratch_shapes=[
            VMEM((particles, width), f32),
            VMEM((owned, particles, TILE), f32),
            VMEM((owned, particles, TILE), bf16),
            pltpu.SemaphoreType.DMA,
        ],
        compiler_params=params(6),
    )(column, positions, incoming)
    fetched_new = exchange(outgoing, "dp")
    everyone = [moved]
    for ahead in range(1, groups):
        ring = [(g, (g + ahead) % groups) for g in range(groups)]
        everyone.append(lax.ppermute(moved, "dom", ring))
    sums = pl.pallas_call(
        likelihood_kernel,
        out_shape=jax.ShapeDtypeStruct((data_width, 1, TILE), f32),
        in_specs=[sspec(), hspec(), vspec(), vspec(), vspec()],
        out_specs=vspec(),
        scratch_shapes=[VMEM(design.shape, bf16), pltpu.SemaphoreType.DMA((CHUNKS,))],
        compiler_params=params(12),
    )(slot, design, fetched_new, labels, sections)
    sums = exchange(sums, "dp")
    means = pl.pallas_call(
        functools.partial(mean_kernel, particles),
        out_shape=jax.ShapeDtypeStruct((groups, 1, TILE), f32),
        in_specs=[vspec()],
        out_specs=vspec(),
        compiler_params=params(1),
    )(sums)
    table = exchange(means, "dom")[:, 0]
    advanced = pl.pallas_call(
        pick_kernel,
        out_shape=jax.ShapeDtypeStruct((particles, width), f32),
        in_specs=[sspec(), sspec()] + [vspec()] * groups,
        out_specs=vspec(),
        scratch_shapes=[VMEM((groups * particles, width), f32), pltpu.SemaphoreType.DMA((groups,))],
        compiler_params=params(4),
    )(group, ancestors, *everyone)
    from_group = jnp.arange(groups)[None, :, None] == (ancestors // particles)[:, None, None]
    from_row = jnp.arange(TILE)[None, None, :] == (ancestors % particles)[:, None, None]
    means = jnp.sum(jnp.where(from_group & from_row, table[None], 0.0), axis=(1, 2))
    return advanced, means


def solution(mesh):
    return jax.shard_map(
        shards,
        mesh=mesh,
        in_specs=(P("dom", "dp"), P("dom"), P(), P("dp", None), P("dp", None), P("dp"), P("dp")),
        out_specs=(P("dom", "dp"), P("dom")),
        check_vma=False,
    )
```

```python
import functools

import jax
import jax.numpy as jnp
from jax import lax
from jax.experimental import pallas as pl
from jax.experimental.pallas import tpu as pltpu
from jax.sharding import PartitionSpec as P


TILE = 128
CURRENT = 2
CHUNKS = 4
COST = 1 << 30
step_size = 1.0
prior_precision = 0.05

f32 = jnp.float32
bf16 = jnp.bfloat16
f16 = jnp.float16

VMEM = pltpu.VMEM
SMEM = pltpu.SMEM


def vspec():
    return pl.BlockSpec(memory_space=VMEM)


def sspec():
    return pl.BlockSpec(memory_space=SMEM)


def hspec():
    return pl.BlockSpec(memory_space=pltpu.HBM)


def params(mib):
    return pltpu.CompilerParams(vmem_limit_bytes=mib << 20)


def exchange(x, axes):
    return lax.all_to_all(x, axes, split_axis=0, concat_axis=0, tiled=True)


def select_kernel(me, choice, positions, outgoing, column, choice_here, here, blocks, sems):
    first = pltpu.make_async_copy(choice, choice_here, sems.at[0])
    second = pltpu.make_async_copy(positions, here, sems.at[1])
    first.start()
    second.start()
    second.wait()
    for q in range(blocks.shape[0]):
        blocks[q] = here[:, q * TILE : (q + 1) * TILE].astype(bf16)
    first.wait()

    def send(d, carry):
        chosen = choice_here[d, me[0]]
        column[d] = chosen
        outgoing[d] = blocks[chosen]
        return carry

    lax.fori_loop(0, outgoing.shape[0], send, 0, unroll=8)


def weights_of(slot, fetched, b, per_block):
    return jnp.concatenate([fetched[slot[k, b]] for k in range(per_block)], axis=1)


def logits_of(weights, tiles):
    return lax.dot_general(
        weights, tiles, (((1,), (1,)), ((), ())), preferred_element_type=f32
    )


def chunk_copies(design, held, sems):
    chunks = sems.shape[0]
    rows = design.shape[0] // chunks
    return [
        pltpu.make_async_copy(
            design.at[pl.ds(c * rows, rows)], held.at[pl.ds(c * rows, rows)], sems.at[c]
        )
        for c in range(chunks)
    ]


def gradient_kernel(slot, held, fetched, labels, sections, outgoing):
    per_block, row_blocks = slot.shape
    outgoing[...] = jnp.zeros_like(outgoing)

    def tiles_of(b):
        return held[b * TILE : (b + 1) * TILE, :]

    residuals = []
    for b in range(row_blocks):
        logits = logits_of(weights_of(slot, fetched, b, per_block), tiles_of(b))
        target = labels[b : b + 1, :].astype(f32)
        active = sections[b : b + 1, :] <= CURRENT
        residual = jnp.where(active, target - jax.nn.sigmoid(logits), 0.0)
        residuals.append(residual.astype(bf16))
    for b in range(row_blocks):
        terms = jnp.dot(residuals[b], tiles_of(b), preferred_element_type=f32)
        for k in range(per_block):
            j = slot[k, b]
            outgoing[j] += terms[:, k * TILE : (k + 1) * TILE]


def advance_kernel(column, positions, incoming, advanced, outgoing, here, total, blocks, sem):
    copy = pltpu.make_async_copy(positions, here, sem)
    copy.start()
    total[...] = jnp.zeros_like(total)

    def add(s, carry):
        total[column[s]] += incoming[s].astype(f32)
        return carry

    lax.fori_loop(0, incoming.shape[0], add, 0, unroll=4)
    copy.wait()
    for q in range(blocks.shape[0]):
        lanes = slice(q * TILE, (q + 1) * TILE)
        old = here[:, lanes]
        new = old + step_size * (total[q] - prior_precision * old)
        advanced[:, lanes] = new
        blocks[q] = new.astype(bf16)

    def send(d, carry):
        outgoing[d] = blocks[column[d]]
        return carry

    lax.fori_loop(0, outgoing.shape[0], send, 0, unroll=8)


def pick_kernel(group, ancestors, *refs):
    moved, (resampled, table, sems) = refs[:-3], refs[-3:]
    particles = resampled.shape[0]
    groups = len(moved)
    copies = [
        pltpu.make_async_copy(moved[k], table.at[pl.ds(k * particles, particles)], sems.at[k])
        for k in range(groups)
    ]
    for copy in copies:
        copy.start()
    for copy in copies:
        copy.wait()

    def pick(i, carry):
        a = ancestors[i]
        ahead = lax.rem(group[0] - lax.div(a, particles) + groups, groups)
        row = ahead * particles + lax.rem(a, particles)
        resampled[pl.ds(i, 1), :] = table[pl.ds(row, 1), :]
        return carry

    lax.fori_loop(0, particles, pick, 0, unroll=8)


def likelihood_kernel(slot, design, fetched, labels, sections, outgoing, held, sems):
    per_block, row_blocks = slot.shape
    particles = fetched.shape[1]
    copies = chunk_copies(design, held, sems)
    for copy in copies:
        copy.start()
    total = jnp.zeros((particles, TILE), f32)
    counted = jnp.zeros((1, TILE), f32)
    for b in range(row_blocks):
        if b % (row_blocks // len(copies)) == 0:
            copies[b // (row_blocks // len(copies))].wait()
        tiles = held[b * TILE : (b + 1) * TILE, :]
        logits = logits_of(weights_of(slot, fetched, b, per_block), tiles)
        target = labels[b : b + 1, :].astype(f32)
        chosen = sections[b : b + 1, :] == CURRENT + 1
        soft = jnp.maximum(logits, 0.0) + jnp.log1p(jnp.exp(-jnp.abs(logits)))
        total += jnp.where(chosen, target * logits - soft, 0.0)
        counted += chosen.astype(f32)
    rows = jnp.concatenate([total, jnp.broadcast_to(counted, (TILE - particles, TILE))], axis=0)
    sums = jnp.sum(rows.T, axis=0, keepdims=True)
    outgoing[...] = jnp.broadcast_to(sums[None], outgoing.shape)


def mean_kernel(particles, sums, means):
    total = jnp.sum(sums[...], axis=0)
    count = jnp.maximum(total[:, particles : particles + 1], 1.0)
    means[...] = jnp.broadcast_to((total / count)[None], means.shape)


def shards(positions, ancestors, block_choice, tile_slot, design, labels, row_section):
    data_width = lax.axis_size("dp")
    groups = lax.axis_size("dom")
    me = lax.axis_index("dp").astype(jnp.int32).reshape(1)
    group = lax.axis_index("dom").astype(jnp.int32).reshape(1)
    particles, width = positions.shape
    owned = width // TILE
    row_blocks = tile_slot.shape[0]
    labels = labels.reshape(row_blocks, TILE)
    sections = row_section.reshape(row_blocks, TILE)
    block_shape = (data_width, particles, TILE)
    slot = tile_slot.T
    near = design
    design = pltpu.with_memory_space_constraint(design, pltpu.HBM)

    positions = pltpu.with_memory_space_constraint(positions, pltpu.HBM)
    chosen = pltpu.with_memory_space_constraint(block_choice, pltpu.HBM)
    outgoing, column = pl.pallas_call(
        select_kernel,
        out_shape=(
            jax.ShapeDtypeStruct(block_shape, bf16),
            jax.ShapeDtypeStruct((data_width,), jnp.int32),
        ),
        in_specs=[sspec(), hspec(), hspec()],
        out_specs=(vspec(), sspec()),
        scratch_shapes=[
            SMEM(block_choice.shape, jnp.int32),
            VMEM((particles, width), f32),
            VMEM((owned, particles, TILE), bf16),
            pltpu.SemaphoreType.DMA((2,)),
        ],
        cost_estimate=pl.CostEstimate(flops=COST, bytes_accessed=COST, transcendentals=0),
        compiler_params=params(4),
    )(me, chosen, positions)
    fetched = exchange(outgoing, "dp")
    terms = pl.pallas_call(
        gradient_kernel,
        out_shape=jax.ShapeDtypeStruct(block_shape, f32),
        in_specs=[sspec(), vspec(), vspec(), vspec(), vspec()],
        out_specs=vspec(),
        compiler_params=params(8),
    )(slot, near, fetched, labels, sections)
    incoming = exchange(terms.astype(f16), "dp").astype(f32)
    moved, outgoing = pl.pallas_call(
        advance_kernel,
        out_shape=(
            jax.ShapeDtypeStruct((particles, width), f32),
            jax.ShapeDtypeStruct(block_shape, bf16),
        ),
        in_specs=[sspec(), hspec(), vspec()],
        out_specs=(vspec(), vspec()),
        scratch_shapes=[
            VMEM((particles, width), f32),
            VMEM((owned, particles, TILE), f32),
            VMEM((owned, particles, TILE), bf16),
            pltpu.SemaphoreType.DMA,
        ],
        compiler_params=params(6),
    )(column, positions, incoming)
    fetched_new = exchange(outgoing, "dp")
    everyone = [moved]
    for ahead in range(1, groups):
        ring = [(g, (g + ahead) % groups) for g in range(groups)]
        everyone.append(lax.ppermute(moved, "dom", ring))
    sums = pl.pallas_call(
        likelihood_kernel,
        out_shape=jax.ShapeDtypeStruct((data_width, 1, TILE), f32),
        in_specs=[sspec(), hspec(), vspec(), vspec(), vspec()],
        out_specs=vspec(),
        scratch_shapes=[VMEM(design.shape, bf16), pltpu.SemaphoreType.DMA((CHUNKS,))],
        compiler_params=params(12),
    )(slot, design, fetched_new, labels, sections)
    sums = exchange(sums, "dp")
    means = pl.pallas_call(
        functools.partial(mean_kernel, particles),
        out_shape=jax.ShapeDtypeStruct((groups, 1, TILE), f32),
        in_specs=[vspec()],
        out_specs=vspec(),
        compiler_params=params(1),
    )(sums)
    table = exchange(means, "dom")[:, 0]
    advanced = pl.pallas_call(
        pick_kernel,
        out_shape=jax.ShapeDtypeStruct((particles, width), f32),
        in_specs=[sspec(), sspec()] + [vspec()] * groups,
        out_specs=vspec(),
        scratch_shapes=[VMEM((groups * particles, width), f32), pltpu.SemaphoreType.DMA((groups,))],
        compiler_params=params(4),
    )(group, ancestors, *everyone)
    from_group = jnp.arange(groups)[None, :, None] == (ancestors // particles)[:, None, None]
    from_row = jnp.arange(TILE)[None, None, :] == (ancestors % particles)[:, None, None]
    means = jnp.sum(jnp.where(from_group & from_row, table[None], 0.0), axis=(1, 2))
    return advanced, means


def solution(mesh):
    return jax.shard_map(
        shards,
        mesh=mesh,
        in_specs=(P("dom", "dp"), P("dom"), P(), P("dp", None), P("dp", None), P("dp"), P("dp")),
        out_specs=(P("dom", "dp"), P("dom")),
        check_vma=False,
    )
```

```python
import functools

import jax
import jax.numpy as jnp
from jax import lax
from jax.experimental import pallas as pl
from jax.experimental.pallas import tpu as pltpu
from jax.sharding import PartitionSpec as P


TILE = 128
CURRENT = 2
CHUNKS = 4
COST = 1 << 30
step_size = 1.0
prior_precision = 0.05

f32 = jnp.float32
bf16 = jnp.bfloat16
f16 = jnp.float16

VMEM = pltpu.VMEM
SMEM = pltpu.SMEM


def vspec():
    return pl.BlockSpec(memory_space=VMEM)


def sspec():
    return pl.BlockSpec(memory_space=SMEM)


def hspec():
    return pl.BlockSpec(memory_space=pltpu.HBM)


def params(mib):
    return pltpu.CompilerParams(vmem_limit_bytes=mib << 20)


def exchange(x, axes):
    return lax.all_to_all(x, axes, split_axis=0, concat_axis=0, tiled=True)


def select_kernel(me, choice, positions, outgoing, column, choice_here, here, blocks, sems):
    first = pltpu.make_async_copy(choice, choice_here, sems.at[0])
    second = pltpu.make_async_copy(positions, here, sems.at[1])
    first.start()
    second.start()
    second.wait()
    for q in range(blocks.shape[0]):
        blocks[q] = here[:, q * TILE : (q + 1) * TILE].astype(bf16)
    first.wait()

    def send(d, carry):
        chosen = choice_here[d, me[0]]
        column[d] = chosen
        outgoing[d] = blocks[chosen]
        return carry

    lax.fori_loop(0, outgoing.shape[0], send, 0, unroll=8)


def weights_of(slot, fetched, b, per_block):
    return jnp.concatenate([fetched[slot[k, b]] for k in range(per_block)], axis=1)


def logits_of(weights, tiles):
    return lax.dot_general(
        weights, tiles, (((1,), (1,)), ((), ())), preferred_element_type=f32
    )


def chunk_copies(design, held, sems):
    chunks = sems.shape[0]
    rows = design.shape[0] // chunks
    return [
        pltpu.make_async_copy(
            design.at[pl.ds(c * rows, rows)], held.at[pl.ds(c * rows, rows)], sems.at[c]
        )
        for c in range(chunks)
    ]


def gradient_kernel(slot, held, fetched, labels, sections, outgoing):
    per_block, row_blocks = slot.shape
    outgoing[...] = jnp.zeros_like(outgoing)

    def tiles_of(b):
        return held[b * TILE : (b + 1) * TILE, :]

    residuals = []
    for b in range(row_blocks):
        logits = logits_of(weights_of(slot, fetched, b, per_block), tiles_of(b))
        target = labels[b : b + 1, :].astype(f32)
        active = sections[b : b + 1, :] <= CURRENT
        residual = jnp.where(active, target - jax.nn.sigmoid(logits), 0.0)
        residuals.append(residual.astype(bf16))
    for b in range(row_blocks):
        terms = jnp.dot(residuals[b], tiles_of(b), preferred_element_type=f32)
        for k in range(per_block):
            j = slot[k, b]
            outgoing[j] += terms[:, k * TILE : (k + 1) * TILE]


def advance_kernel(column, positions, incoming, advanced, outgoing, here, total, blocks, sem):
    copy = pltpu.make_async_copy(positions, here, sem)
    copy.start()
    total[...] = jnp.zeros_like(total)

    def add(s, carry):
        total[column[s]] += incoming[s].astype(f32)
        return carry

    lax.fori_loop(0, incoming.shape[0], add, 0, unroll=4)
    copy.wait()
    for q in range(blocks.shape[0]):
        lanes = slice(q * TILE, (q + 1) * TILE)
        old = here[:, lanes]
        new = old + step_size * (total[q] - prior_precision * old)
        advanced[:, lanes] = new
        blocks[q] = new.astype(bf16)

    def send(d, carry):
        outgoing[d] = blocks[column[d]]
        return carry

    lax.fori_loop(0, outgoing.shape[0], send, 0, unroll=8)


def pick_kernel(places, group, ancestors, *refs):
    moved, (resampled, table, sems) = refs[:-3], refs[-3:]
    particles = resampled.shape[0]
    groups = len(places)
    copies = [
        pltpu.make_async_copy(
            moved[which].at[pl.ds(part * particles, particles)],
            table.at[pl.ds(ahead * particles, particles)],
            sems.at[ahead],
        )
        for ahead, (which, part) in enumerate(places)
    ]
    for copy in copies:
        copy.start()
    for copy in copies:
        copy.wait()

    def pick(i, carry):
        a = ancestors[i]
        ahead = lax.rem(group[0] - lax.div(a, particles) + groups, groups)
        row = ahead * particles + lax.rem(a, particles)
        resampled[pl.ds(i, 1), :] = table[pl.ds(row, 1), :]
        return carry

    lax.fori_loop(0, particles, pick, 0, unroll=8)


def likelihood_kernel(slot, design, fetched, labels, sections, outgoing, held, sems):
    per_block, row_blocks = slot.shape
    particles = fetched.shape[1]
    copies = chunk_copies(design, held, sems)
    for copy in copies:
        copy.start()
    total = jnp.zeros((particles, TILE), f32)
    counted = jnp.zeros((1, TILE), f32)
    for b in range(row_blocks):
        if b % (row_blocks // len(copies)) == 0:
            copies[b // (row_blocks // len(copies))].wait()
        tiles = held[b * TILE : (b + 1) * TILE, :]
        logits = logits_of(weights_of(slot, fetched, b, per_block), tiles)
        target = labels[b : b + 1, :].astype(f32)
        chosen = sections[b : b + 1, :] == CURRENT + 1
        soft = jnp.maximum(logits, 0.0) + jnp.log1p(jnp.exp(-jnp.abs(logits)))
        total += jnp.where(chosen, target * logits - soft, 0.0)
        counted += chosen.astype(f32)
    rows = jnp.concatenate([total, jnp.broadcast_to(counted, (TILE - particles, TILE))], axis=0)
    sums = jnp.sum(rows.T, axis=0, keepdims=True)
    outgoing[...] = jnp.broadcast_to(sums[None], outgoing.shape)


def mean_kernel(particles, sums, means):
    total = jnp.sum(sums[...], axis=0)
    count = jnp.maximum(total[:, particles : particles + 1], 1.0)
    means[...] = jnp.broadcast_to((total / count)[None], means.shape)


def shards(positions, ancestors, block_choice, tile_slot, design, labels, row_section):
    data_width = lax.axis_size("dp")
    groups = lax.axis_size("dom")
    me = lax.axis_index("dp").astype(jnp.int32).reshape(1)
    group = lax.axis_index("dom").astype(jnp.int32).reshape(1)
    particles, width = positions.shape
    owned = width // TILE
    row_blocks = tile_slot.shape[0]
    labels = labels.reshape(row_blocks, TILE)
    sections = row_section.reshape(row_blocks, TILE)
    block_shape = (data_width, particles, TILE)
    slot = tile_slot.T
    near = design
    design = pltpu.with_memory_space_constraint(design, pltpu.HBM)

    positions = pltpu.with_memory_space_constraint(positions, pltpu.HBM)
    chosen = pltpu.with_memory_space_constraint(block_choice, pltpu.HBM)
    outgoing, column = pl.pallas_call(
        select_kernel,
        out_shape=(
            jax.ShapeDtypeStruct(block_shape, bf16),
            jax.ShapeDtypeStruct((data_width,), jnp.int32),
        ),
        in_specs=[sspec(), hspec(), hspec()],
        out_specs=(vspec(), sspec()),
        scratch_shapes=[
            SMEM(block_choice.shape, jnp.int32),
            VMEM((particles, width), f32),
            VMEM((owned, particles, TILE), bf16),
            pltpu.SemaphoreType.DMA((2,)),
        ],
        cost_estimate=pl.CostEstimate(flops=COST, bytes_accessed=COST, transcendentals=0),
        compiler_params=params(4),
    )(me, chosen, positions)
    fetched = exchange(outgoing, "dp")
    terms = pl.pallas_call(
        gradient_kernel,
        out_shape=jax.ShapeDtypeStruct(block_shape, f32),
        in_specs=[sspec(), vspec(), vspec(), vspec(), vspec()],
        out_specs=vspec(),
        compiler_params=params(8),
    )(slot, near, fetched, labels, sections)
    incoming = exchange(terms.astype(f16), "dp").astype(f32)
    moved, outgoing = pl.pallas_call(
        advance_kernel,
        out_shape=(
            jax.ShapeDtypeStruct((particles, width), f32),
            jax.ShapeDtypeStruct(block_shape, bf16),
        ),
        in_specs=[sspec(), hspec(), vspec()],
        out_specs=(vspec(), vspec()),
        scratch_shapes=[
            VMEM((particles, width), f32),
            VMEM((owned, particles, TILE), f32),
            VMEM((owned, particles, TILE), bf16),
            pltpu.SemaphoreType.DMA,
        ],
        compiler_params=params(6),
    )(column, positions, incoming)
    fetched_new = exchange(outgoing, "dp")

    def turn(x, ahead):
        return lax.ppermute(x, "dom", [(g, (g + ahead) % groups) for g in range(groups)])

    assert groups == 8
    below = turn(moved, 1)
    above = turn(moved, 7)
    three = jnp.concatenate([moved, below, above], axis=0)
    further = turn(three, 3)
    back = turn(three, 6)
    everyone = [moved, below, above, further, back]
    places = [(0, 0), (1, 0), (3, 2), (3, 0), (3, 1), (4, 2), (4, 0), (2, 0)]
    sums = pl.pallas_call(
        likelihood_kernel,
        out_shape=jax.ShapeDtypeStruct((data_width, 1, TILE), f32),
        in_specs=[sspec(), hspec(), vspec(), vspec(), vspec()],
        out_specs=vspec(),
        scratch_shapes=[VMEM(design.shape, bf16), pltpu.SemaphoreType.DMA((CHUNKS,))],
        compiler_params=params(12),
    )(slot, design, fetched_new, labels, sections)
    sums = exchange(sums, "dp")
    means = pl.pallas_call(
        functools.partial(mean_kernel, particles),
        out_shape=jax.ShapeDtypeStruct((groups, 1, TILE), f32),
        in_specs=[vspec()],
        out_specs=vspec(),
        compiler_params=params(1),
    )(sums)
    table = exchange(means, "dom")[:, 0]
    advanced = pl.pallas_call(
        functools.partial(pick_kernel, places),
        out_shape=jax.ShapeDtypeStruct((particles, width), f32),
        in_specs=[sspec(), sspec()] + [vspec()] * len(everyone),
        out_specs=vspec(),
        scratch_shapes=[VMEM((groups * particles, width), f32), pltpu.SemaphoreType.DMA((groups,))],
        compiler_params=params(4),
    )(group, ancestors, *everyone)
    from_group = jnp.arange(groups)[None, :, None] == (ancestors // particles)[:, None, None]
    from_row = jnp.arange(TILE)[None, None, :] == (ancestors % particles)[:, None, None]
    means = jnp.sum(jnp.where(from_group & from_row, table[None], 0.0), axis=(1, 2))
    return advanced, means


def solution(mesh):
    return jax.shard_map(
        shards,
        mesh=mesh,
        in_specs=(P("dom", "dp"), P("dom"), P(), P("dp", None), P("dp", None), P("dp"), P("dp")),
        out_specs=(P("dom", "dp"), P("dom")),
        check_vma=False,
    )
```
